32 devices in a mesh: groups: 2 (over y), row: 4 (over x, core), col: 4 (over z).
Axes of the slice: x: 2, y: 2, z: 4, core: 2. Of those that a mesh axis runs over, the one named last changes fastest.
Arguments:
- inputs: bfloat16 [1536, 4096], P(('groups', 'col'), 'row'), parts along dimension 0, may hold values from -6 to 6
- cotangent: bfloat16 [1536, 4096], P(('groups', 'col'), 'row'), parts along dimension 0, may hold values from -6 to 6
- preactivation: bfloat16 [1536, 8192], P(('groups', 'row'), 'col'), parts along dimension 0, may hold values from -8 to 8
- up_weight: bfloat16 [4096, 8192], P('row', 'col'), may hold values from -0.09375 to 0.09375
- down_weight: bfloat16 [8192, 4096], P('col', 'row'), may hold values from -0.0625 to 0.0625
Outputs:
- grad_input: bfloat16 [1536, 4096], P(('groups', 'col'), 'row'), parts along dimension 0
- grad_up: float32 [8192, 8192], P(('groups', 'row'), 'col'), parts along dimension 0
- grad_down: float32 [16384, 4096], P(('groups', 'col'), 'row'), parts along dimension 0
The draws below stay inside these ranges and needn't reach their ends.
There are 2 independent parts, one for each index of `groups`. The reference program is written for one: setup_inputs(seed, part) draws one part's arguments, and reference() takes and returns one part's arrays. A program takes and returns all parts, laid end to end along the dimension named above; an argument that names none is the same for every part. Nothing has to cross between parts.
All inputs are finite; a program needn't handle non-finite values.
Results may differ from the reference program's by a relative error of at most 0.0049.
Values may be sent and summed in bfloat16 or wider, within the bound.
A program may use at most 128 MiB of HBM per device.

```python
import jax
import jax.numpy as jnp

D = 4096
H = 8192
TOKENS = 768


def block_scale(key, extent, cuts, smallest, top_value):
    level, own = 1.0, jax.random.fold_in(key, 6)
    for axis_at, blocks in cuts:
        draws = jnp.exp(jax.random.uniform(jax.random.fold_in(own, axis_at), (blocks,), jnp.float32, smallest / len(cuts), top_value / len(cuts)))
        level = level * jnp.repeat(draws, extent[axis_at] // blocks).reshape([-1 if axis == axis_at else 1 for axis in range(len(extent))])
    return level


def scatter_about(own_key, shape, deviation, reach, pieces=(), dtype=jnp.bfloat16):
    result = jax.random.normal(own_key, shape, jnp.float32) * deviation
    if len(pieces) > 0:
        result = block_scale(own_key, shape, pieces, -0.22, 0.18) * result
    return jnp.clip(result, min=-reach, max=reach).astype(dtype)


def setup_inputs(seed: int = 0, part: int = 0) -> dict:
    key_list = jax.random.split(jax.random.key(seed), 6)
    part_keys = jax.random.split(jax.random.fold_in(key_list[5], part), 6)
    return {
        "inputs": scatter_about(part_keys[0], (TOKENS, D), 1.0, 6.0, ((0, 4), (1, 4))),
        "cotangent": scatter_about(part_keys[1], (TOKENS, D), 1.0, 6.0, ((0, 4), (1, 4))),
        "preactivation": scatter_about(part_keys[2], (TOKENS, H), 1.5, 8.0, ((0, 4), (1, 4))),
        "up_weight": scatter_about(key_list[3], (D, H), D ** -0.5, 0.09375, ((0, 4), (1, 4))),
        "down_weight": scatter_about(key_list[4], (H, D), H ** -0.5, 0.0625, ((0, 4), (1, 4))),
    }


def gelu_pair(values):
    v = values.astype(jnp.float32)
    tanh_arg = 0.7978845608 * (v + 0.044715 * v * v * v)
    tanh_val = jnp.tanh(tanh_arg)
    gelu_value = 0.5 * v * (1.0 + tanh_val)
    gelu_slope = 0.5 * (1.0 + tanh_val) + 0.5 * v * (1.0 - tanh_val * tanh_val) * 0.7978845608 * (1.0 + 3.0 * 0.044715 * v * v)
    return gelu_value, gelu_slope


def reference(inputs, cotangent, preactivation, up_weight, down_weight):
    hidden_grad = jnp.dot(cotangent, down_weight.T, preferred_element_type=jnp.float32)
    gelu_value, gelu_slope = gelu_pair(preactivation)
    activation = gelu_value.astype(jnp.bfloat16)
    pre_grad = (hidden_grad * gelu_slope).astype(jnp.bfloat16)
    grad_input = jnp.dot(pre_grad, up_weight.T, preferred_element_type=jnp.float32).astype(jnp.bfloat16)
    token_scale = 1.0 / (TOKENS ** 0.5)
    grad_up = jnp.dot(inputs.T, pre_grad, preferred_element_type=jnp.float32) * token_scale
    grad_down = jnp.dot(activation.T, cotangent, preferred_element_type=jnp.float32) * token_scale
    return grad_input, grad_up, grad_down
```

```python
import functools
import math

import jax
import jax.numpy as jnp
from jax import lax
from jax.experimental import pallas as pl
from jax.experimental.pallas import tpu as pltpu
from jax.sharding import PartitionSpec as P

F32, BF16 = jnp.float32, jnp.bfloat16
LAST = (((1,), (1,)), ((), ()))
FIRST = (((0,), (0,)), ((), ()))


def tanh_of(v):
    return jnp.tanh(0.7978845608 * (v + 0.044715 * v * v * v))


def gelu_value(values):
    v = values.astype(F32)
    return 0.5 * v * (1.0 + tanh_of(v))


def gelu_slope(values):
    v = values.astype(F32)
    t = tanh_of(v)
    return 0.5 * (1.0 + t) + 0.5 * v * (1.0 - t * t) * 0.7978845608 * (1.0 + 3.0 * 0.044715 * v * v)


def remote(src, dst, send, recv, where):
    return pltpu.make_async_remote_copy(
        src_ref=src, dst_ref=dst, send_sem=send, recv_sem=recv, device_id=where,
        device_id_type=pl.DeviceIdType.MESH,
    )


def block_at(c, t, nc):
    near = jnp.minimum(c, nc - 1 - c)
    step = -((t + 1) // 2) if t % 2 else t // 2
    return jnp.where(t <= 2 * near, c + step, jnp.where(2 * c < nc - 1, t, nc - 1 - t))


def kernel(
    nr, nc,
    x_ref, cot_ref, pre_ref, up_ref, down_ref,
    gi_ref, x_out, cot_out, act_out, pg_out,
    x_all, cot_all, pre_all, act_all, pg_all, up, down, part, h1_out, h1_in, h2_out, h2_in,
    gi_own, gi_out, gi_in,
    loc, cot_s, cot_r, x_s, x_r, pre_s, pre_r, h1_s, h1_r, h2_s, h2_r, pg_s, pg_r, gi_s, gi_r,
):
    r, c = lax.axis_index("row"), lax.axis_index("col")
    nx = nr // 2
    x, k = r // 2, r % 2
    mate = {"row": 2 * x + (1 - k)}
    tb, dr = gi_ref.shape
    ts, hc = pg_all.shape[1:]
    hb, db, eb = min(512, hc), min(512, dr), min(256, hc)
    peers = [(x + d) % nx for d in range(1, nx)]
    ends = []

    barrier = pltpu.get_barrier_semaphore()
    pl.semaphore_signal(barrier, inc=1, device_id=mate, device_id_type=pl.DeviceIdType.MESH)
    for p in peers:
        pl.semaphore_signal(barrier, inc=1, device_id={"row": 2 * p + k}, device_id_type=pl.DeviceIdType.MESH)
    for d in range(1, nc):
        pl.semaphore_signal(barrier, inc=1, device_id={"col": (c + d) % nc}, device_id_type=pl.DeviceIdType.MESH)
    local = [
        pltpu.make_async_copy(cot_ref, cot_all.at[c], loc.at[0]),
        pltpu.make_async_copy(down_ref, down, loc.at[1]),
        pltpu.make_async_copy(pre_ref, pre_all.at[pl.ds(r * nc, nc)], loc.at[2]),
        pltpu.make_async_copy(up_ref, up, loc.at[3]),
        pltpu.make_async_copy(x_ref, x_all.at[c], loc.at[4]),
    ]
    for copy in local:
        copy.start()
    pl.semaphore_wait(barrier, nx + nc - 1)

    def line(all_ref, send, recv, direction, j, source):
        return remote(source, all_ref.at[j], send.at[direction, j], recv.at[j],
                      {"col": c + 1 if direction == 0 else c - 1})

    def pass_on(all_ref, send, recv, own_ref, t):
        for direction, j in ((0, c - t), (1, c + t)):
            there = (j >= 0) & (j < nc)
            onward = (c + 1 < nc) if direction == 0 else (c >= 1)
            jj = jnp.clip(j, 0, nc - 1)
            if t > 0:
                @pl.when(there)
                def _():
                    line(all_ref, send, recv, direction, jj, all_ref.at[jj]).wait_recv()

            @pl.when(there & onward)
            def _():
                src = own_ref if t == 0 else all_ref.at[jj]
                line(all_ref, send, recv, direction, jj, src).start()

    def finish_line(all_ref, send, recv):
        for t in range(nc):
            for direction, j in ((0, c - t), (1, c + t)):
                onward = (c + 1 < nc) if direction == 0 else (c >= 1)
                jj = jnp.clip(j, 0, nc - 1)

                @pl.when((j >= 0) & (j < nc) & onward)
                def _():
                    line(all_ref, send, recv, direction, jj, all_ref.at[jj]).wait_send()

    def pre_copy(index, source_row, target_row, src=None):
        units = pre_all.at[pl.ds(source_row * nc, nc)]
        return remote(units if src is None else src, units, pre_s.at[index], pre_r.at[source_row],
                      {"row": target_row})

    def started(copy):
        copy.start()
        ends.append(copy)

    mate_row = 2 * x + (1 - k)
    pass_on(cot_all, cot_s, cot_r, cot_ref, 0)
    for i, p in enumerate(peers):
        started(pre_copy(1 + i, r, 2 * p + k, pre_ref))
    started(pre_copy(0, r, mate_row, pre_ref))

    def activate(row):
        steps = hc // eb

        def body(i, _):
            unit, at = row * nc + i // steps, pl.ds(pl.multiple_of((i % steps) * eb, eb), eb)
            act_all[unit, :, at] = gelu_value(pre_all[unit, :, at]).astype(BF16)
            return 0

        lax.fori_loop(0, nc * steps, body, 0)

    def s0(t):
        j = block_at(c, t, nc)
        if t == 0:
            local[0].wait()
            local[1].wait()
        block = cot_all[j]

        def body(i, _):
            at = pl.ds(pl.multiple_of(i * hb, hb), hb)
            got = lax.dot_general(block, down[at, :], LAST, preferred_element_type=F32)
            for s in range(nr):
                part[t, s, :, at] = got[s * ts : (s + 1) * ts]
            return 0

        lax.fori_loop(0, hc // hb, body, 0)
        for p in range(nx):
            h1_out[t, p] = part[t, 2 * p + (1 - k)].astype(BF16)
        started(remote(h1_out.at[t], h1_in.at[t], h1_s.at[t], h1_r.at[t], mate))

    def s1(t):
        remote(h1_out.at[t], h1_in.at[t], h1_s.at[t], h1_r.at[t], mate).wait_recv()
        for i, p in enumerate(peers):
            h2_out[t, i] = (part[t, 2 * p + k] + h1_in[t, p].astype(F32)).astype(BF16)
            started(remote(h2_out.at[t, i], h2_in.at[t, i], h2_s.at[t, i], h2_r.at[t, i],
                           {"row": 2 * p + k}))

    def pg_copy(t, index, source_row, target_row):
        unit = pg_all.at[block_at(c, t, nc) * nr + source_row]
        return remote(unit, unit, pg_s.at[t, index], pg_r.at[t, source_row], {"row": target_row})

    def s2(t):
        for i, p in enumerate(peers):
            remote(h2_out.at[t, i], h2_in.at[t, i], h2_s.at[t, i], h2_r.at[t, i],
                   {"row": 2 * p + k}).wait_recv()
        unit = block_at(c, t, nc) * nr + r

        def body(i, _):
            at = pl.ds(pl.multiple_of(i * eb, eb), eb)
            total = part[t, 2 * x + k, :, at] + h1_in[t, x, :, at].astype(F32)
            for i in range(nx - 1):
                total += h2_in[t, i, :, at].astype(F32)
            pg_all[unit, :, at] = (total * gelu_slope(pre_all[unit, :, at])).astype(BF16)
            return 0

        lax.fori_loop(0, hc // eb, body, 0)
        for i, p in enumerate(peers):
            started(pg_copy(t, 1 + i, r, 2 * p + k))
        started(pg_copy(t, 0, r, mate_row))

    def s3(t):
        for i, p in enumerate(peers):
            pg_copy(t, 0, 2 * p + k, mate_row).wait_recv()
            started(pg_copy(t, nx + i, 2 * p + k, mate_row))

    def gi_copy(j, source):
        return remote(gi_out.at[j], gi_in.at[source], gi_s.at[j], gi_r.at[source], {"col": j})

    def s4(t):
        j = block_at(c, t, nc)
        for p in range(nx):
            pg_copy(t, 0, 2 * p + (1 - k), mate_row).wait_recv()
        if t == 0:
            local[3].wait()
        units = pg_all[pl.ds(j * nr, nr)]

        def put(at, rows, got):
            if t == 0:
                gi_own[rows, at] = got
            else:
                gi_out[j, rows, at] = got.astype(BF16)

        def body(i, _):
            at = pl.ds(pl.multiple_of(i * db, db), db)
            if ts % 16 == 0:
                put(at, slice(None), lax.dot_general(
                    units.reshape(tb, hc), up[at, :], LAST, preferred_element_type=F32))
            else:
                got = [lax.dot_general(units[s], up[at, :], LAST, preferred_element_type=F32)
                       for s in range(nr)]
                put(at, slice(None), jnp.concatenate(got, axis=0))
            return 0

        lax.fori_loop(0, dr // db, body, 0)
        if t > 0:
            started(gi_copy(j, c))

    def out_copy(src, dst, index):
        copy = pltpu.make_async_copy(src, dst, loc.at[index])
        copy.start()
        outs.append(copy)

    outs = []
    for step in range(nc + 3):
        if 0 <= step - 2 < nc:
            s3(step - 2)
        if step < nc:
            if step > 0:
                pass_on(cot_all, cot_s, cot_r, cot_ref, step)
            s0(step)
            if step == 0:
                local[2].wait()
                activate(r)
            s1(step)
            if step == 0:
                pre_copy(0, mate_row, mate_row).wait_recv()
                activate(mate_row)
            if step == min(1, nc - 1):
                for i, p in enumerate(peers):
                    pre_copy(0, 2 * p + k, mate_row).wait_recv()
                    started(pre_copy(nx + i, 2 * p + k, mate_row))
                for p in peers:
                    pre_copy(0, 2 * p + (1 - k), mate_row).wait_recv()
            if step == nc - 1:
                out_copy(cot_all, cot_out, 5)
                local[4].wait()
                pass_on(x_all, x_s, x_r, x_ref, 0)
        if 0 <= step - 1 < nc:
            s2(step - 1)
        if 0 <= step - 2 < nc:
            s4(step - 2)
        if step == 2:
            for p in peers:
                activate(2 * p + k)
        if step == min(3, nc - 1):
            for p in peers:
                activate(2 * p + 1 - k)
            out_copy(act_all, act_out, 6)
        if step == nc + 1:
            out_copy(pg_all, pg_out, 7)
        if nc <= step < nc + nc - 1:
            pass_on(x_all, x_s, x_r, x_ref, step - nc + 1)
    for t in range(4, nc):
        pass_on(x_all, x_s, x_r, x_ref, t)
    out_copy(x_all, x_out, 8)
    total = gi_own[...]
    for d in range(1, nc):
        source = (c + d) % nc
        gi_copy(c, source).wait_recv()
        total += gi_in[source].astype(F32)
    gi_ref[...] = total.astype(BF16)
    for copy in ends:
        copy.wait_send()
    finish_line(cot_all, cot_s, cot_r)
    finish_line(x_all, x_s, x_r)
    for copy in outs:
        copy.wait()


def per_device(nr, nc, inputs, cotangent, preactivation, up_weight, down_weight):
    tb, dr = inputs.shape
    hc = up_weight.shape[1]
    ts, nx = tb // nr, nr // 2
    tokens = tb * nc
    dma = pltpu.SemaphoreType.DMA
    anywhere = pl.BlockSpec(memory_space=pl.ANY)
    shape = jax.ShapeDtypeStruct
    grad_input, x_all, cot_all, act_all, pg_all = pl.pallas_call(
        functools.partial(kernel, nr, nc),
        out_shape=(
            shape((tb, dr), BF16), shape((nc, tb, dr), BF16), shape((nc, tb, dr), BF16),
            shape((nc * nr, ts, hc), BF16), shape((nc * nr, ts, hc), BF16),
        ),
        in_specs=[anywhere] * 5,
        out_specs=(pl.BlockSpec(memory_space=pltpu.VMEM),) + (anywhere,) * 4,
        scratch_shapes=[
            pltpu.VMEM((nc, tb, dr), BF16), pltpu.VMEM((nc, tb, dr), BF16),
            pltpu.VMEM((nc * nr, ts, hc), BF16), pltpu.VMEM((nc * nr, ts, hc), BF16),
            pltpu.VMEM((nc * nr, ts, hc), BF16),
            pltpu.VMEM(up_weight.shape, BF16), pltpu.VMEM(down_weight.shape, BF16),
            pltpu.VMEM((nc, nr, ts, hc), F32),
            pltpu.VMEM((nc, nx, ts, hc), BF16), pltpu.VMEM((nc, nx, ts, hc), BF16),
            pltpu.VMEM((nc, nx - 1, ts, hc), BF16), pltpu.VMEM((nc, nx - 1, ts, hc), BF16),
            pltpu.VMEM((tb, dr), F32),
            pltpu.VMEM((nc, tb, dr), BF16), pltpu.VMEM((nc, tb, dr), BF16),
            dma((9,)), dma((2, nc)), dma((nc,)), dma((2, nc)), dma((nc,)),
            dma((2 * nx,)), dma((nr,)), dma((nc,)), dma((nc,)),
            dma((nc, nx - 1)), dma((nc, nx - 1)), dma((nc, 2 * nx)), dma((nc, nr)),
            dma((nc,)), dma((nc,)),
        ],
        compiler_params=pltpu.CompilerParams(
            collective_id=0, has_side_effects=True, vmem_limit_bytes=60 * 1024 * 1024
        ),
    )(inputs, cotangent, preactivation.reshape(nc, ts, hc), up_weight, down_weight)
    token_scale = 1.0 / math.sqrt(tokens)
    x_all, cot_all = x_all.reshape(tokens, dr), cot_all.reshape(tokens, dr)
    act_all, pg_all = act_all.reshape(tokens, hc), pg_all.reshape(tokens, hc)
    grad_up = lax.dot_general(x_all, pg_all, FIRST, preferred_element_type=F32) * token_scale
    grad_down = lax.dot_general(act_all, cot_all, FIRST, preferred_element_type=F32) * token_scale
    return (grad_input, grad_up, grad_down)


def solution(mesh):
    placed = (
        P(("groups", "col"), "row"),
        P(("groups", "col"), "row"),
        P(("groups", "row"), "col"),
        P("row", "col"),
        P("col", "row"),
    )
    return jax.shard_map(
        functools.partial(per_device, mesh.shape["row"], mesh.shape["col"]),
        mesh=mesh,
        in_specs=placed,
        out_specs=(
            P(("groups", "col"), "row"),
            P(("groups", "row"), "col"),
            P(("groups", "col"), "row"),
        ),
        check_vma=False,
    )
```

```python
import functools
import math

import jax
import jax.numpy as jnp
from jax import lax
from jax.experimental import pallas as pl
from jax.experimental.pallas import tpu as pltpu
from jax.sharding import PartitionSpec as P

F32, BF16 = jnp.float32, jnp.bfloat16
LAST = (((1,), (1,)), ((), ()))
FIRST = (((0,), (0,)), ((), ()))


def tanh_of(v):
    return jnp.tanh(0.7978845608 * (v + 0.044715 * v * v * v))


def gelu_value(values):
    v = values.astype(F32)
    return 0.5 * v * (1.0 + tanh_of(v))


def gelu_slope(values):
    v = values.astype(F32)
    t = tanh_of(v)
    return 0.5 * (1.0 + t) + 0.5 * v * (1.0 - t * t) * 0.7978845608 * (1.0 + 3.0 * 0.044715 * v * v)


def remote(src, dst, send, recv, where):
    return pltpu.make_async_remote_copy(
        src_ref=src, dst_ref=dst, send_sem=send, recv_sem=recv, device_id=where,
        device_id_type=pl.DeviceIdType.MESH,
    )


def block_at(c, t, nc):
    near = jnp.minimum(c, nc - 1 - c)
    step = -((t + 1) // 2) if t % 2 else t // 2
    return jnp.where(t <= 2 * near, c + step, jnp.where(2 * c < nc - 1, t, nc - 1 - t))


def kernel(
    nr, nc,
    x_ref, cot_ref, pre_ref, up_ref, down_ref,
    gi_ref, x_out, cot_out, act_out, pg_out,
    x_all, cot_all, pre_all, act_all, pg_all, up, down, part, h1_out, h1_in, h2_out, h2_in,
    gi_own, gi_out, gi_in,
    loc, cot_s, cot_r, x_s, x_r, pre_s, pre_r, h1_s, h1_r, h2_s, h2_r, pg_s, pg_r, gi_s, gi_r,
):
    r, c = lax.axis_index("row"), lax.axis_index("col")
    nx = nr // 2
    x, k = r // 2, r % 2
    mate = {"row": 2 * x + (1 - k)}
    tb, dr = gi_ref.shape
    ts, hc = pg_all.shape[1:]
    hb, db, eb = min(512, hc), min(512, dr), min(256, hc)
    peers = [(x + d) % nx for d in range(1, nx)]
    ends = []

    barrier = pltpu.get_barrier_semaphore()
    pl.semaphore_signal(barrier, inc=1, device_id=mate, device_id_type=pl.DeviceIdType.MESH)
    for p in peers:
        pl.semaphore_signal(barrier, inc=1, device_id={"row": 2 * p + k}, device_id_type=pl.DeviceIdType.MESH)
    for d in range(1, nc):
        pl.semaphore_signal(barrier, inc=1, device_id={"col": (c + d) % nc}, device_id_type=pl.DeviceIdType.MESH)
    local = [
        pltpu.make_async_copy(cot_ref, cot_all.at[c], loc.at[0]),
        pltpu.make_async_copy(down_ref, down, loc.at[1]),
        pltpu.make_async_copy(pre_ref, pre_all.at[pl.ds(r * nc, nc)], loc.at[2]),
        pltpu.make_async_copy(up_ref, up, loc.at[3]),
        pltpu.make_async_copy(x_ref, x_all.at[c], loc.at[4]),
    ]
    for copy in local:
        copy.start()
    pl.semaphore_wait(barrier, nx + nc - 1)

    def line(all_ref, send, recv, direction, j, source):
        return remote(source, all_ref.at[j], send.at[direction, j], recv.at[j],
                      {"col": c + 1 if direction == 0 else c - 1})

    def pass_on(all_ref, send, recv, own_ref, t):
        for direction, j in ((0, c - t), (1, c + t)):
            there = (j >= 0) & (j < nc)
            onward = (c + 1 < nc) if direction == 0 else (c >= 1)
            jj = jnp.clip(j, 0, nc - 1)
            if t > 0:
                @pl.when(there)
                def _():
                    line(all_ref, send, recv, direction, jj, all_ref.at[jj]).wait_recv()

            @pl.when(there & onward)
            def _():
                src = own_ref if t == 0 else all_ref.at[jj]
                line(all_ref, send, recv, direction, jj, src).start()

    def finish_line(all_ref, send, recv):
        for t in range(nc):
            for direction, j in ((0, c - t), (1, c + t)):
                onward = (c + 1 < nc) if direction == 0 else (c >= 1)
                jj = jnp.clip(j, 0, nc - 1)

                @pl.when((j >= 0) & (j < nc) & onward)
                def _():
                    line(all_ref, send, recv, direction, jj, all_ref.at[jj]).wait_send()

    def pre_copy(index, source_row, target_row, src=None):
        units = pre_all.at[pl.ds(source_row * nc, nc)]
        return remote(units if src is None else src, units, pre_s.at[index], pre_r.at[source_row],
                      {"row": target_row})

    def started(copy):
        copy.start()
        ends.append(copy)

    mate_row = 2 * x + (1 - k)
    pass_on(cot_all, cot_s, cot_r, cot_ref, 0)
    for i, p in enumerate(peers):
        started(pre_copy(1 + i, r, 2 * p + k, pre_ref))
    started(pre_copy(0, r, mate_row, pre_ref))

    def activate(row):
        steps = hc // eb

        def body(i, _):
            unit, at = row * nc + i // steps, pl.ds(pl.multiple_of((i % steps) * eb, eb), eb)
            act_all[unit, :, at] = gelu_value(pre_all[unit, :, at]).astype(BF16)
            return 0

        lax.fori_loop(0, nc * steps, body, 0)

    def s0(t):
        j = block_at(c, t, nc)
        if t == 0:
            local[0].wait()
            local[1].wait()
        block = cot_all[j]

        def body(i, _):
            at = pl.ds(pl.multiple_of(i * hb, hb), hb)
            got = lax.dot_general(block, down[at, :], LAST, preferred_element_type=F32)
            for s in range(nr):
                part[t, s, :, at] = got[s * ts : (s + 1) * ts]
            return 0

        lax.fori_loop(0, hc // hb, body, 0)
        for p in range(nx):
            h1_out[t, p] = part[t, 2 * p + (1 - k)].astype(BF16)
        started(remote(h1_out.at[t], h1_in.at[t], h1_s.at[t], h1_r.at[t], mate))

    def s1(t):
        remote(h1_out.at[t], h1_in.at[t], h1_s.at[t], h1_r.at[t], mate).wait_recv()
        for i, p in enumerate(peers):
            h2_out[t, i] = (part[t, 2 * p + k] + h1_in[t, p].astype(F32)).astype(BF16)
            started(remote(h2_out.at[t, i], h2_in.at[t, i], h2_s.at[t, i], h2_r.at[t, i],
                           {"row": 2 * p + k}))

    def pg_copy(t, index, source_row, target_row):
        unit = pg_all.at[block_at(c, t, nc) * nr + source_row]
        return remote(unit, unit, pg_s.at[t, index], pg_r.at[t, source_row], {"row": target_row})

    def s2(t):
        for i, p in enumerate(peers):
            remote(h2_out.at[t, i], h2_in.at[t, i], h2_s.at[t, i], h2_r.at[t, i],
                   {"row": 2 * p + k}).wait_recv()
        unit = block_at(c, t, nc) * nr + r

        def body(i, _):
            at = pl.ds(pl.multiple_of(i * eb, eb), eb)
            total = part[t, 2 * x + k, :, at] + h1_in[t, x, :, at].astype(F32)
            for i in range(nx - 1):
                total += h2_in[t, i, :, at].astype(F32)
            pg_all[unit, :, at] = (total * gelu_slope(pre_all[unit, :, at])).astype(BF16)
            return 0

        lax.fori_loop(0, hc // eb, body, 0)
        for i, p in enumerate(peers):
            started(pg_copy(t, 1 + i, r, 2 * p + k))
        started(pg_copy(t, 0, r, mate_row))

    def s3(t):
        for i, p in enumerate(peers):
            pg_copy(t, 0, 2 * p + k, mate_row).wait_recv()
            started(pg_copy(t, nx + i, 2 * p + k, mate_row))

    def gi_copy(j, source):
        return remote(gi_out.at[j], gi_in.at[source], gi_s.at[j], gi_r.at[source], {"col": j})

    def s4(t):
        j = block_at(c, t, nc)
        for p in range(nx):
            pg_copy(t, 0, 2 * p + (1 - k), mate_row).wait_recv()
        units = pg_all[pl.ds(j * nr, nr)]

        def put(at, rows, got):
            if t == 0:
                gi_own[rows, at] = got
            else:
                gi_out[j, rows, at] = got.astype(BF16)

        def body(i, _):
            at = pl.ds(pl.multiple_of(i * db, db), db)
            if ts % 16 == 0:
                put(at, slice(None), lax.dot_general(
                    units.reshape(tb, hc), up[at, :], LAST, preferred_element_type=F32))
            else:
                got = [lax.dot_general(units[s], up[at, :], LAST, preferred_element_type=F32)
                       for s in range(nr)]
                put(at, slice(None), jnp.concatenate(got, axis=0))
            return 0

        lax.fori_loop(0, dr // db, body, 0)
        if t > 0:
            started(gi_copy(j, c))

    def out_copy(src, dst, index):
        copy = pltpu.make_async_copy(src, dst, loc.at[index])
        copy.start()
        outs.append(copy)

    outs = []

    def x_on(step):
        for direction, far in ((0, c), (1, nc - 1 - c)):
            t = step - far
            j = c - t if direction == 0 else c + t
            jj = jnp.clip(j, 0, nc - 1)
            fits = (t >= 0) & (t <= far) & (far < nc - 1)

            @pl.when(fits & (t > 0))
            def _():
                line(x_all, x_s, x_r, direction, jj, x_all.at[jj]).wait_recv()

            @pl.when(fits)
            def _():
                line(x_all, x_s, x_r, direction, jj, x_all.at[jj]).start()

    def x_rest():
        for direction, far in ((0, c), (1, nc - 1 - c)):
            for t in range(1, nc):
                j = c - t if direction == 0 else c + t

                @pl.when((far == nc - 1))
                def _():
                    jj = jnp.clip(j, 0, nc - 1)
                    line(x_all, x_s, x_r, direction, jj, x_all.at[jj]).wait_recv()

    local[4].wait()
    for step in range(nc):
        if step == 1:
            local[3].wait()
        if step > 0:
            pass_on(cot_all, cot_s, cot_r, cot_ref, step)
        x_on(step)
        s0(step)
        if step == 0:
            local[2].wait()
            activate(r)
        s1(step)
        if step == 0:
            pre_copy(0, mate_row, mate_row).wait_recv()
            activate(mate_row)
        if step == min(2, nc - 1):
            for i, p in enumerate(peers):
                pre_copy(0, 2 * p + k, mate_row).wait_recv()
                started(pre_copy(nx + i, 2 * p + k, mate_row))
            for p in peers:
                pre_copy(0, 2 * p + (1 - k), mate_row).wait_recv()
        if step >= 2:
            s2(step - 2)
        if step >= 3:
            s3(step - 3)
    out_copy(cot_all, cot_out, 5)
    onward = list(range(nc, 2 * nc - 3))
    for at in onward[:1]:
        x_on(at)
    s2(nc - 2)
    for p in peers:
        activate(2 * p + k)
    s3(nc - 3)
    s2(nc - 1)
    for t in range(1, nc - 2):
        s4(t)
    for at in onward[1:]:
        x_on(at)
    for p in peers:
        activate(2 * p + 1 - k)
    out_copy(act_all, act_out, 6)
    s3(nc - 2)
    s4(nc - 2)
    s4(0)
    s3(nc - 1)
    s4(nc - 1)
    out_copy(pg_all, pg_out, 7)
    x_rest()
    out_copy(x_all, x_out, 8)
    total = gi_own[...]
    for d in range(1, nc):
        source = (c + d) % nc
        gi_copy(c, source).wait_recv()
        total += gi_in[source].astype(F32)
    gi_ref[...] = total.astype(BF16)
    for copy in ends:
        copy.wait_send()
    finish_line(cot_all, cot_s, cot_r)
    finish_line(x_all, x_s, x_r)
    for copy in outs:
        copy.wait()


def per_device(nr, nc, inputs, cotangent, preactivation, up_weight, down_weight):
    tb, dr = inputs.shape
    hc = up_weight.shape[1]
    ts, nx = tb // nr, nr // 2
    tokens = tb * nc
    dma = pltpu.SemaphoreType.DMA
    anywhere = pl.BlockSpec(memory_space=pl.ANY)
    shape = jax.ShapeDtypeStruct
    grad_input, x_all, cot_all, act_all, pg_all = pl.pallas_call(
        functools.partial(kernel, nr, nc),
        out_shape=(
            shape((tb, dr), BF16), shape((nc, tb, dr), BF16), shape((nc, tb, dr), BF16),
            shape((nc * nr, ts, hc), BF16), shape((nc * nr, ts, hc), BF16),
        ),
        in_specs=[anywhere] * 5,
        out_specs=(pl.BlockSpec(memory_space=pltpu.VMEM),) + (anywhere,) * 4,
        scratch_shapes=[
            pltpu.VMEM((nc, tb, dr), BF16), pltpu.VMEM((nc, tb, dr), BF16),
            pltpu.VMEM((nc * nr, ts, hc), BF16), pltpu.VMEM((nc * nr, ts, hc), BF16),
            pltpu.VMEM((nc * nr, ts, hc), BF16),
            pltpu.VMEM(up_weight.shape, BF16), pltpu.VMEM(down_weight.shape, BF16),
            pltpu.VMEM((nc, nr, ts, hc), F32),
            pltpu.VMEM((nc, nx, ts, hc), BF16), pltpu.VMEM((nc, nx, ts, hc), BF16),
            pltpu.VMEM((nc, nx - 1, ts, hc), BF16), pltpu.VMEM((nc, nx - 1, ts, hc), BF16),
            pltpu.VMEM((tb, dr), F32),
            pltpu.VMEM((nc, tb, dr), BF16), pltpu.VMEM((nc, tb, dr), BF16),
            dma((9,)), dma((2, nc)), dma((nc,)), dma((2, nc)), dma((nc,)),
            dma((2 * nx,)), dma((nr,)), dma((nc,)), dma((nc,)),
            dma((nc, nx - 1)), dma((nc, nx - 1)), dma((nc, 2 * nx)), dma((nc, nr)),
            dma((nc,)), dma((nc,)),
        ],
        compiler_params=pltpu.CompilerParams(
            collective_id=0, has_side_effects=True, vmem_limit_bytes=60 * 1024 * 1024
        ),
    )(inputs, cotangent, preactivation.reshape(nc, ts, hc), up_weight, down_weight)
    token_scale = 1.0 / math.sqrt(tokens)
    x_all, cot_all = x_all.reshape(tokens, dr), cot_all.reshape(tokens, dr)
    act_all, pg_all = act_all.reshape(tokens, hc), pg_all.reshape(tokens, hc)
    grad_up = lax.dot_general(x_all, pg_all, FIRST, preferred_element_type=F32) * token_scale
    grad_down = lax.dot_general(act_all, cot_all, FIRST, preferred_element_type=F32) * token_scale
    return (grad_input, grad_up, grad_down)


def solution(mesh):
    placed = (
        P(("groups", "col"), "row"),
        P(("groups", "col"), "row"),
        P(("groups", "row"), "col"),
        P("row", "col"),
        P("col", "row"),
    )
    return jax.shard_map(
        functools.partial(per_device, mesh.shape["row"], mesh.shape["col"]),
        mesh=mesh,
        in_specs=placed,
        out_specs=(
            P(("groups", "col"), "row"),
            P(("groups", "row"), "col"),
            P(("groups", "col"), "row"),
        ),
        check_vma=False,
    )
```

```python
import functools
import math

import jax
import jax.numpy as jnp
from jax import lax
from jax.experimental import pallas as pl
from jax.experimental.pallas import tpu as pltpu
from jax.sharding import PartitionSpec as P

F32, BF16 = jnp.float32, jnp.bfloat16
LAST = (((1,), (1,)), ((), ()))
FIRST = (((0,), (0,)), ((), ()))


def tanh_of(v):
    return jnp.tanh(0.7978845608 * (v + 0.044715 * v * v * v))


def gelu_value(values):
    v = values.astype(F32)
    return 0.5 * v * (1.0 + tanh_of(v))


def gelu_slope(values):
    v = values.astype(F32)
    t = tanh_of(v)
    return 0.5 * (1.0 + t) + 0.5 * v * (1.0 - t * t) * 0.7978845608 * (1.0 + 3.0 * 0.044715 * v * v)


def remote(src, dst, send, recv, where):
    return pltpu.make_async_remote_copy(
        src_ref=src, dst_ref=dst, send_sem=send, recv_sem=recv, device_id=where,
        device_id_type=pl.DeviceIdType.MESH,
    )


def block_at(c, t, nc):
    near = jnp.minimum(c, nc - 1 - c)
    step = -((t + 1) // 2) if t % 2 else t // 2
    return jnp.where(t <= 2 * near, c + step, jnp.where(2 * c < nc - 1, t, nc - 1 - t))


def kernel(
    nr, nc,
    x_ref, cot_ref, pre_ref, up_ref, down_ref,
    gi_ref, x_out, cot_out, act_out, pg_out,
    x_all, cot_all, pre_all, act_all, pg_all, up, down, part, h1_out, h1_in, h2_out, h2_in,
    gi_own, gi_out, gi_in,
    loc, cot_s, cot_r, x_s, x_r, pre_s, pre_r, act_s, act_r, h1_s, h1_r, h2_s, h2_r, pg_s, pg_r, gi_s, gi_r,
):
    r, c = lax.axis_index("row"), lax.axis_index("col")
    nx = nr // 2
    x, k = r // 2, r % 2
    mate = {"row": 2 * x + (1 - k)}
    tb, dr = gi_ref.shape
    ts, hc = pg_all.shape[1:]
    hb, db, eb = min(512, hc), min(512, dr), min(256, hc)
    peers = [(x + d) % nx for d in range(1, nx)]
    ends = []

    barrier = pltpu.get_barrier_semaphore()
    for d in range(1, nr):
        pl.semaphore_signal(barrier, inc=1, device_id={"row": (r + d) % nr}, device_id_type=pl.DeviceIdType.MESH)
    for d in range(1, nc):
        pl.semaphore_signal(barrier, inc=1, device_id={"col": (c + d) % nc}, device_id_type=pl.DeviceIdType.MESH)
    local = [
        pltpu.make_async_copy(cot_ref, cot_all.at[c], loc.at[0]),
        pltpu.make_async_copy(down_ref, down, loc.at[1]),
        pltpu.make_async_copy(pre_ref, pre_all.at[pl.ds(r * nc, nc)], loc.at[2]),
        pltpu.make_async_copy(up_ref, up, loc.at[3]),
        pltpu.make_async_copy(x_ref, x_all.at[c], loc.at[4]),
    ]
    for copy in local:
        copy.start()
    pl.semaphore_wait(barrier, nr + nc - 2)

    def line(all_ref, send, recv, direction, j, source):
        return remote(source, all_ref.at[j], send.at[direction, j], recv.at[j],
                      {"col": c + 1 if direction == 0 else c - 1})

    def pass_on(all_ref, send, recv, own_ref, t):
        for direction, j in ((0, c - t), (1, c + t)):
            there = (j >= 0) & (j < nc)
            onward = (c + 1 < nc) if direction == 0 else (c >= 1)
            jj = jnp.clip(j, 0, nc - 1)
            if t > 0:
                @pl.when(there)
                def _():
                    line(all_ref, send, recv, direction, jj, all_ref.at[jj]).wait_recv()

            @pl.when(there & onward)
            def _():
                src = own_ref if t == 0 else all_ref.at[jj]
                line(all_ref, send, recv, direction, jj, src).start()

    def finish_line(all_ref, send, recv):
        for t in range(nc):
            for direction, j in ((0, c - t), (1, c + t)):
                onward = (c + 1 < nc) if direction == 0 else (c >= 1)
                jj = jnp.clip(j, 0, nc - 1)

                @pl.when((j >= 0) & (j < nc) & onward)
                def _():
                    line(all_ref, send, recv, direction, jj, all_ref.at[jj]).wait_send()

    def act_copy(index, source_row, target_row):
        units = act_all.at[pl.ds(source_row * nc, nc)]
        return remote(units, units, act_s.at[index], act_r.at[source_row], {"row": target_row})

    def pre_copy(i):
        unit = r * nc + i
        return remote(pre_ref.at[i], pre_all.at[unit], pre_s.at[i], pre_r.at[unit // nr],
                      {"row": unit % nr}), unit % nr != r

    def started(copy):
        copy.start()
        ends.append(copy)

    mate_row = 2 * x + (1 - k)
    pass_on(cot_all, cot_s, cot_r, cot_ref, 0)
    for i in range(nc):
        copy, away = pre_copy(i)
        pl.when(away)(copy.start)

    def activate(row):
        steps = hc // eb

        def body(i, _):
            unit, at = row * nc + i // steps, pl.ds(pl.multiple_of((i % steps) * eb, eb), eb)
            act_all[unit, :, at] = gelu_value(pre_all[unit, :, at]).astype(BF16)
            return 0

        lax.fori_loop(0, nc * steps, body, 0)

    def s0(t):
        j = block_at(c, t, nc)
        if t == 0:
            local[0].wait()
            local[1].wait()
        block = cot_all[j]

        def body(i, _):
            at = pl.ds(pl.multiple_of(i * hb, hb), hb)
            got = lax.dot_general(block, down[at, :], LAST, preferred_element_type=F32)
            for s in range(nr):
                part[t, s, :, at] = got[s * ts : (s + 1) * ts]
            return 0

        lax.fori_loop(0, hc // hb, body, 0)
        for p in range(nx):
            h1_out[t, p] = part[t, 2 * p + (1 - k)].astype(BF16)
        started(remote(h1_out.at[t], h1_in.at[t], h1_s.at[t], h1_r.at[t], mate))

    def s1(t):
        remote(h1_out.at[t], h1_in.at[t], h1_s.at[t], h1_r.at[t], mate).wait_recv()
        for i, p in enumerate(peers):
            h2_out[t, i] = (part[t, 2 * p + k] + h1_in[t, p].astype(F32)).astype(BF16)
            started(remote(h2_out.at[t, i], h2_in.at[t, i], h2_s.at[t, i], h2_r.at[t, i],
                           {"row": 2 * p + k}))

    def pg_copy(t, index, source_row, target_row):
        unit = pg_all.at[block_at(c, t, nc) * nr + source_row]
        return remote(unit, unit, pg_s.at[t, index], pg_r.at[t, source_row], {"row": target_row})

    def s2(t):
        for i, p in enumerate(peers):
            remote(h2_out.at[t, i], h2_in.at[t, i], h2_s.at[t, i], h2_r.at[t, i],
                   {"row": 2 * p + k}).wait_recv()
        j = block_at(c, t, nc)
        unit = j * nr + r

        @pl.when(unit // nc != r)
        def _():
            remote(pre_ref.at[0], pre_all.at[unit], pre_s.at[0], pre_r.at[j], mate).wait_recv()

        def body(i, _):
            at = pl.ds(pl.multiple_of(i * eb, eb), eb)
            total = part[t, 2 * x + k, :, at] + h1_in[t, x, :, at].astype(F32)
            for i in range(nx - 1):
                total += h2_in[t, i, :, at].astype(F32)
            pg_all[unit, :, at] = (total * gelu_slope(pre_all[unit, :, at])).astype(BF16)
            return 0

        lax.fori_loop(0, hc // eb, body, 0)
        for i, p in enumerate(peers):
            started(pg_copy(t, 1 + i, r, 2 * p + k))
        started(pg_copy(t, 0, r, mate_row))

    def s3(t):
        for i, p in enumerate(peers):
            pg_copy(t, 0, 2 * p + k, mate_row).wait_recv()
            started(pg_copy(t, nx + i, 2 * p + k, mate_row))

    def gi_copy(j, source):
        return remote(gi_out.at[j], gi_in.at[source], gi_s.at[j], gi_r.at[source], {"col": j})

    def s4(t):
        j = block_at(c, t, nc)
        for p in range(nx):
            pg_copy(t, 0, 2 * p + (1 - k), mate_row).wait_recv()
        units = pg_all[pl.ds(j * nr, nr)]

        def put(at, rows, got):
            if t == 0:
                gi_own[rows, at] = got
            else:
                gi_out[j, rows, at] = got.astype(BF16)

        def body(i, _):
            at = pl.ds(pl.multiple_of(i * db, db), db)
            if ts % 16 == 0:
                put(at, slice(None), lax.dot_general(
                    units.reshape(tb, hc), up[at, :], LAST, preferred_element_type=F32))
            else:
                got = [lax.dot_general(units[s], up[at, :], LAST, preferred_element_type=F32)
                       for s in range(nr)]
                put(at, slice(None), jnp.concatenate(got, axis=0))
            return 0

        lax.fori_loop(0, dr // db, body, 0)
        if t > 0:
            started(gi_copy(j, c))

    def out_copy(src, dst, index):
        copy = pltpu.make_async_copy(src, dst, loc.at[index])
        copy.start()
        outs.append(copy)

    outs = []

    def x_on(step):
        for direction, far in ((0, c), (1, nc - 1 - c)):
            t = step - far
            j = c - t if direction == 0 else c + t
            jj = jnp.clip(j, 0, nc - 1)
            fits = (t >= 0) & (t <= far) & (far < nc - 1)

            @pl.when(fits & (t > 0))
            def _():
                line(x_all, x_s, x_r, direction, jj, x_all.at[jj]).wait_recv()

            @pl.when(fits)
            def _():
                line(x_all, x_s, x_r, direction, jj, x_all.at[jj]).start()

    def x_rest():
        for direction, far in ((0, c), (1, nc - 1 - c)):
            for t in range(1, nc):
                j = c - t if direction == 0 else c + t

                @pl.when((far == nc - 1))
                def _():
                    jj = jnp.clip(j, 0, nc - 1)
                    line(x_all, x_s, x_r, direction, jj, x_all.at[jj]).wait_recv()

    local[4].wait()
    for step in range(nc):
        if step == 1:
            local[3].wait()
        if step > 0:
            pass_on(cot_all, cot_s, cot_r, cot_ref, step)
        x_on(step)
        s0(step)
        if step == 0:
            local[2].wait()
            activate(r)
        s1(step)
        if step >= 1:
            s2(step - 1)
        if step >= 2:
            s3(step - 2)
    out_copy(cot_all, cot_out, 5)
    onward = list(range(nc, 2 * nc - 3))
    for at in onward[:1]:
        x_on(at)
    for t in range(1, nc - 2):
        s4(t)
    s2(nc - 1)
    for i, p in enumerate(peers):
        started(act_copy(1 + i, r, 2 * p + k))
    started(act_copy(0, r, mate_row))
    s3(nc - 2)
    s4(nc - 2)
    for at in onward[1:]:
        x_on(at)
    s4(0)
    s3(nc - 1)
    s4(nc - 1)
    for i, p in enumerate(peers):
        act_copy(0, 2 * p + k, mate_row).wait_recv()
        started(act_copy(nx + i, 2 * p + k, mate_row))
    for p in range(nx):
        act_copy(0, 2 * p + 1 - k, mate_row).wait_recv()
    out_copy(act_all, act_out, 6)
    out_copy(pg_all, pg_out, 7)
    x_rest()
    out_copy(x_all, x_out, 8)
    total = gi_own[...]
    for d in range(1, nc):
        source = (c + d) % nc
        gi_copy(c, source).wait_recv()
        total += gi_in[source].astype(F32)
    gi_ref[...] = total.astype(BF16)
    for copy in ends:
        copy.wait_send()
    for i in range(nc):
        copy, away = pre_copy(i)
        pl.when(away)(copy.wait_send)
    finish_line(cot_all, cot_s, cot_r)
    finish_line(x_all, x_s, x_r)
    for copy in outs:
        copy.wait()


def per_device(nr, nc, inputs, cotangent, preactivation, up_weight, down_weight):
    tb, dr = inputs.shape
    hc = up_weight.shape[1]
    ts, nx = tb // nr, nr // 2
    tokens = tb * nc
    dma = pltpu.SemaphoreType.DMA
    anywhere = pl.BlockSpec(memory_space=pl.ANY)
    shape = jax.ShapeDtypeStruct
    grad_input, x_all, cot_all, act_all, pg_all = pl.pallas_call(
        functools.partial(kernel, nr, nc),
        out_shape=(
            shape((tb, dr), BF16), shape((nc, tb, dr), BF16), shape((nc, tb, dr), BF16),
            shape((nc * nr, ts, hc), BF16), shape((nc * nr, ts, hc), BF16),
        ),
        in_specs=[anywhere] * 5,
        out_specs=(pl.BlockSpec(memory_space=pltpu.VMEM),) + (anywhere,) * 4,
        scratch_shapes=[
            pltpu.VMEM((nc, tb, dr), BF16), pltpu.VMEM((nc, tb, dr), BF16),
            pltpu.VMEM((nc * nr, ts, hc), BF16), pltpu.VMEM((nc * nr, ts, hc), BF16),
            pltpu.VMEM((nc * nr, ts, hc), BF16),
            pltpu.VMEM(up_weight.shape, BF16), pltpu.VMEM(down_weight.shape, BF16),
            pltpu.VMEM((nc, nr, ts, hc), F32),
            pltpu.VMEM((nc, nx, ts, hc), BF16), pltpu.VMEM((nc, nx, ts, hc), BF16),
            pltpu.VMEM((nc, nx - 1, ts, hc), BF16), pltpu.VMEM((nc, nx - 1, ts, hc), BF16),
            pltpu.VMEM((tb, dr), F32),
            pltpu.VMEM((nc, tb, dr), BF16), pltpu.VMEM((nc, tb, dr), BF16),
            dma((9,)), dma((2, nc)), dma((nc,)), dma((2, nc)), dma((nc,)),
            dma((nc,)), dma((nc,)), dma((2 * nx,)), dma((nr,)), dma((nc,)), dma((nc,)),
            dma((nc, nx - 1)), dma((nc, nx - 1)), dma((nc, 2 * nx)), dma((nc, nr)),
            dma((nc,)), dma((nc,)),
        ],
        compiler_params=pltpu.CompilerParams(
            collective_id=0, has_side_effects=True, vmem_limit_bytes=60 * 1024 * 1024
        ),
    )(inputs, cotangent, preactivation.reshape(nc, ts, hc), up_weight, down_weight)
    token_scale = 1.0 / math.sqrt(tokens)
    x_all, cot_all = x_all.reshape(tokens, dr), cot_all.reshape(tokens, dr)
    act_all, pg_all = act_all.reshape(tokens, hc), pg_all.reshape(tokens, hc)
    grad_up = lax.dot_general(x_all, pg_all, FIRST, preferred_element_type=F32) * token_scale
    grad_down = lax.dot_general(act_all, cot_all, FIRST, preferred_element_type=F32) * token_scale
    return (grad_input, grad_up, grad_down)


def solution(mesh):
    placed = (
        P(("groups", "col"), "row"),
        P(("groups", "col"), "row"),
        P(("groups", "row"), "col"),
        P("row", "col"),
        P("col", "row"),
    )
    return jax.shard_map(
        functools.partial(per_device, mesh.shape["row"], mesh.shape["col"]),
        mesh=mesh,
        in_specs=placed,
        out_specs=(
            P(("groups", "col"), "row"),
            P(("groups", "row"), "col"),
            P(("groups", "col"), "row"),
        ),
        check_vma=False,
    )
```

```python
import functools
import math

import jax
import jax.numpy as jnp
from jax import lax
from jax.experimental import pallas as pl
from jax.experimental.pallas import tpu as pltpu
from jax.sharding import PartitionSpec as P


F32, BF16 = jnp.float32, jnp.bfloat16
LAST = (((1,), (1,)), ((), ()))
FIRST = (((0,), (0,)), ((), ()))


def tanh_of(v):
    return jnp.tanh(0.7978845608 * (v + 0.044715 * v * v * v))


def gelu_value(values):
    v = values.astype(F32)
    return 0.5 * v * (1.0 + tanh_of(v))


def gelu_slope(values):
    v = values.astype(F32)
    t = tanh_of(v)
    return 0.5 * (1.0 + t) + 0.5 * v * (1.0 - t * t) * 0.7978845608 * (1.0 + 3.0 * 0.044715 * v * v)


def remote(src, dst, send, recv, where):
    return pltpu.make_async_remote_copy(
        src_ref=src, dst_ref=dst, send_sem=send, recv_sem=recv, device_id=where,
        device_id_type=pl.DeviceIdType.MESH,
    )


def block_at(c, t, nc):
    near = jnp.minimum(c, nc - 1 - c)
    step = -((t + 1) // 2) if t % 2 else t // 2
    return jnp.where(t <= 2 * near, c + step, jnp.where(2 * c < nc - 1, t, nc - 1 - t))


def kernel(
    nr, nc,
    x_ref, cot_ref, pre_ref, up_ref, down_ref,
    *rest,
):
    gi_ref, x_out, cot_out, act_out, pg_out, *gi_outs = rest[: 4 + nc]
    (
    x_all, cot_all, pre_all, act_all, pg_all, up, down, part, h1_out, h1_in, h2_out, h2_in,
    gi_own, gi_out,
    loc, cot_s, cot_r, x_s, x_r, pre_s, pre_r, act_s, act_r, h1_s, h1_r, h2_s, h2_r, pg_s, pg_r,
    ) = rest[4 + nc :]
    r, c = lax.axis_index("row"), lax.axis_index("col")
    nx = nr // 2
    x, k = r // 2, r % 2
    mate = {"row": 2 * x + (1 - k)}
    tb, dr = gi_ref.shape
    ts, hc = pg_all.shape[1:]
    hb, db, eb = min(512, hc), min(512, dr), min(256, hc)
    peers = [(x + d) % nx for d in range(1, nx)]
    ends = []

    barrier = pltpu.get_barrier_semaphore()
    for d in range(1, nr):
        pl.semaphore_signal(barrier, inc=1, device_id={"row": (r + d) % nr}, device_id_type=pl.DeviceIdType.MESH)
    for d in range(1, nc):
        pl.semaphore_signal(barrier, inc=1, device_id={"col": (c + d) % nc}, device_id_type=pl.DeviceIdType.MESH)
    local = [
        pltpu.make_async_copy(cot_ref, cot_all.at[c], loc.at[0]),
        pltpu.make_async_copy(down_ref, down, loc.at[1]),
        pltpu.make_async_copy(pre_ref, pre_all.at[pl.ds(r * nc, nc)], loc.at[2]),
        pltpu.make_async_copy(up_ref, up, loc.at[3]),
        pltpu.make_async_copy(x_ref, x_all.at[c], loc.at[4]),
    ]
    for copy in local:
        copy.start()
    pl.semaphore_wait(barrier, nr + nc - 2)

    def line(all_ref, send, recv, direction, j, source):
        return remote(source, all_ref.at[j], send.at[direction, j], recv.at[j],
                      {"col": c + 1 if direction == 0 else c - 1})

    def pass_on(all_ref, send, recv, own_ref, t):
        for direction, j in ((0, c - t), (1, c + t)):
            there = (j >= 0) & (j < nc)
            onward = (c + 1 < nc) if direction == 0 else (c >= 1)
            jj = jnp.clip(j, 0, nc - 1)
            if t > 0:
                @pl.when(there)
                def _():
                    line(all_ref, send, recv, direction, jj, all_ref.at[jj]).wait_recv()

            @pl.when(there & onward)
            def _():
                src = own_ref if t == 0 else all_ref.at[jj]
                line(all_ref, send, recv, direction, jj, src).start()

    def finish_line(all_ref, send, recv):
        for t in range(nc):
            for direction, j in ((0, c - t), (1, c + t)):
                onward = (c + 1 < nc) if direction == 0 else (c >= 1)
                jj = jnp.clip(j, 0, nc - 1)

                @pl.when((j >= 0) & (j < nc) & onward)
                def _():
                    line(all_ref, send, recv, direction, jj, all_ref.at[jj]).wait_send()

    def act_copy(i, index, source_row, target_row):
        unit = act_all.at[source_row * nc + i]
        return remote(unit, unit, act_s.at[i, index], act_r.at[i, source_row], {"row": target_row})

    def act_send(i):
        for n, p in enumerate(peers):
            started(act_copy(i, 1 + n, r, 2 * p + k))
        started(act_copy(i, 0, r, mate_row))

    def act_on(i):
        for n, p in enumerate(peers):
            act_copy(i, 0, 2 * p + k, mate_row).wait_recv()
            started(act_copy(i, nx + n, 2 * p + k, mate_row))

    def pre_copy(i):
        unit = r * nc + i
        return remote(pre_ref.at[i], pre_all.at[unit], pre_s.at[i], pre_r.at[unit // nr],
                      {"row": unit % nr}), unit % nr != r

    def started(copy):
        copy.start()
        ends.append(copy)

    mate_row = 2 * x + (1 - k)
    pass_on(cot_all, cot_s, cot_r, cot_ref, 0)
    for i in range(nc):
        copy, away = pre_copy(i)
        pl.when(away)(copy.start)

    def activate(row):
        steps = hc // eb

        def body(i, _):
            unit, at = row * nc + i // steps, pl.ds(pl.multiple_of((i % steps) * eb, eb), eb)
            act_all[unit, :, at] = gelu_value(pre_all[unit, :, at]).astype(BF16)
            return 0

        lax.fori_loop(0, nc * steps, body, 0)

    def s0(t):
        j = block_at(c, t, nc)
        if t == 0:
            local[0].wait()
            local[1].wait()
        block = cot_all[j]

        def body(i, _):
            at = pl.ds(pl.multiple_of(i * hb, hb), hb)
            got = lax.dot_general(block, down[at, :], LAST, preferred_element_type=F32)
            for s in range(nr):
                part[t, s, :, at] = got[s * ts : (s + 1) * ts]
            return 0

        lax.fori_loop(0, hc // hb, body, 0)
        for p in range(nx):
            h1_out[t, p] = part[t, 2 * p + (1 - k)].astype(BF16)
        started(remote(h1_out.at[t], h1_in.at[t], h1_s.at[t], h1_r.at[t], mate))

    def s1(t):
        remote(h1_out.at[t], h1_in.at[t], h1_s.at[t], h1_r.at[t], mate).wait_recv()
        for i, p in enumerate(peers):
            h2_out[t, i] = (part[t, 2 * p + k] + h1_in[t, p].astype(F32)).astype(BF16)
            started(remote(h2_out.at[t, i], h2_in.at[t, i], h2_s.at[t, i], h2_r.at[t, i],
                           {"row": 2 * p + k}))

    def pg_copy(t, index, source_row, target_row):
        unit = pg_all.at[block_at(c, t, nc) * nr + source_row]
        return remote(unit, unit, pg_s.at[t, index], pg_r.at[t, source_row], {"row": target_row})

    def s2(t):
        for i, p in enumerate(peers):
            remote(h2_out.at[t, i], h2_in.at[t, i], h2_s.at[t, i], h2_r.at[t, i],
                   {"row": 2 * p + k}).wait_recv()
        j = block_at(c, t, nc)
        unit = j * nr + r

        @pl.when(unit // nc != r)
        def _():
            remote(pre_ref.at[0], pre_all.at[unit], pre_s.at[0], pre_r.at[j], mate).wait_recv()

        def body(i, _):
            at = pl.ds(pl.multiple_of(i * eb, eb), eb)
            total = part[t, 2 * x + k, :, at] + h1_in[t, x, :, at].astype(F32)
            for i in range(nx - 1):
                total += h2_in[t, i, :, at].astype(F32)
            pg_all[unit, :, at] = (total * gelu_slope(pre_all[unit, :, at])).astype(BF16)
            return 0

        lax.fori_loop(0, hc // eb, body, 0)
        for i, p in enumerate(peers):
            started(pg_copy(t, 1 + i, r, 2 * p + k))
        started(pg_copy(t, 0, r, mate_row))

    def s3(t):
        for i, p in enumerate(peers):
            pg_copy(t, 0, 2 * p + k, mate_row).wait_recv()
            started(pg_copy(t, nx + i, 2 * p + k, mate_row))

    def s4(t):
        j = block_at(c, t, nc)
        for p in range(nx):
            pg_copy(t, 0, 2 * p + (1 - k), mate_row).wait_recv()
        units = pg_all[pl.ds(j * nr, nr)]

        def put(at, rows, got):
            if t == 0:
                gi_own[rows, at] = got
            else:
                gi_out[(j - c + nc) % nc, rows, at] = got.astype(BF16)

        def body(i, _):
            at = pl.ds(pl.multiple_of(i * db, db), db)
            if ts % 16 == 0:
                put(at, slice(None), lax.dot_general(
                    units.reshape(tb, hc), up[at, :], LAST, preferred_element_type=F32))
            else:
                got = [lax.dot_general(units[s], up[at, :], LAST, preferred_element_type=F32)
                       for s in range(nr)]
                put(at, slice(None), jnp.concatenate(got, axis=0))
            return 0

        lax.fori_loop(0, dr // db, body, 0)

    def out_copy(src, dst, index):
        copy = pltpu.make_async_copy(src, dst, loc.at[index])
        copy.start()
        outs.append(copy)

    outs = []

    def x_on(step):
        for direction, far in ((0, c), (1, nc - 1 - c)):
            t = step - far
            j = c - t if direction == 0 else c + t
            jj = jnp.clip(j, 0, nc - 1)
            fits = (t >= 0) & (t <= far) & (far < nc - 1)

            @pl.when(fits & (t > 0))
            def _():
                line(x_all, x_s, x_r, direction, jj, x_all.at[jj]).wait_recv()

            @pl.when(fits)
            def _():
                line(x_all, x_s, x_r, direction, jj, x_all.at[jj]).start()

    def x_rest():
        for direction, far in ((0, c), (1, nc - 1 - c)):
            for t in range(1, nc):
                j = c - t if direction == 0 else c + t

                @pl.when((far == nc - 1))
                def _():
                    jj = jnp.clip(j, 0, nc - 1)
                    line(x_all, x_s, x_r, direction, jj, x_all.at[jj]).wait_recv()

    early = nc // 2
    local[4].wait()
    for step in range(nc):
        if step == 1:
            local[3].wait()
        if step > 0:
            pass_on(cot_all, cot_s, cot_r, cot_ref, step)
        x_on(step)
        s0(step)
        if step == 0:
            local[2].wait()
            activate(r)
        s1(step)
        if step >= 1:
            s2(step - 1)
        if step < early:
            act_send(step)
        if step >= 2:
            s3(step - 2)
    out_copy(cot_all, cot_out, 5)
    onward = list(range(nc, 2 * nc - 3))
    for at in onward[:1]:
        x_on(at)
    for t in range(1, nc - 2):
        s4(t)
    s2(nc - 1)
    for i in range(early, nc):
        act_send(i)
    s3(nc - 2)
    s4(nc - 2)
    for at in onward[1:]:
        x_on(at)
    s4(0)
    s3(nc - 1)
    s4(nc - 1)
    for d in range(1, nc):
        out_copy(gi_out.at[d], gi_outs[d - 1], 8 + d)
    for i in range(nc):
        act_on(i)
    for i in range(nc):
        for p in range(nx):
            act_copy(i, 0, 2 * p + 1 - k, mate_row).wait_recv()
    out_copy(act_all, act_out, 6)
    out_copy(pg_all, pg_out, 7)
    x_rest()
    out_copy(x_all, x_out, 8)
    gi_ref[...] = gi_own[...]
    for copy in ends:
        copy.wait_send()
    for i in range(nc):
        copy, away = pre_copy(i)
        pl.when(away)(copy.wait_send)
    finish_line(cot_all, cot_s, cot_r)
    finish_line(x_all, x_s, x_r)
    for copy in outs:
        copy.wait()


def per_device(nr, nc, inputs, cotangent, preactivation, up_weight, down_weight):
    tb, dr = inputs.shape
    hc = up_weight.shape[1]
    ts, nx = tb // nr, nr // 2
    tokens = tb * nc
    dma = pltpu.SemaphoreType.DMA
    anywhere = pl.BlockSpec(memory_space=pl.ANY)
    shape = jax.ShapeDtypeStruct
    own, x_all, cot_all, act_all, pg_all, *pieces = pl.pallas_call(
        functools.partial(kernel, nr, nc),
        out_shape=(
            shape((tb, dr), F32), shape((nc, tb, dr), BF16), shape((nc, tb, dr), BF16),
            shape((nc * nr, ts, hc), BF16), shape((nc * nr, ts, hc), BF16),
        ) + (shape((tb, dr), BF16),) * (nc - 1),
        in_specs=[anywhere] * 5,
        out_specs=(pl.BlockSpec(memory_space=pltpu.VMEM),) + (anywhere,) * (3 + nc),
        scratch_shapes=[
            pltpu.VMEM((nc, tb, dr), BF16), pltpu.VMEM((nc, tb, dr), BF16),
            pltpu.VMEM((nc * nr, ts, hc), BF16), pltpu.VMEM((nc * nr, ts, hc), BF16),
            pltpu.VMEM((nc * nr, ts, hc), BF16),
            pltpu.VMEM(up_weight.shape, BF16), pltpu.VMEM(down_weight.shape, BF16),
            pltpu.VMEM((nc, nr, ts, hc), F32),
            pltpu.VMEM((nc, nx, ts, hc), BF16), pltpu.VMEM((nc, nx, ts, hc), BF16),
            pltpu.VMEM((nc, nx - 1, ts, hc), BF16), pltpu.VMEM((nc, nx - 1, ts, hc), BF16),
            pltpu.VMEM((tb, dr), F32),
            pltpu.VMEM((nc, tb, dr), BF16),
            dma((8 + nc,)), dma((2, nc)), dma((nc,)), dma((2, nc)), dma((nc,)),
            dma((nc,)), dma((nc,)), dma((nc, 2 * nx)), dma((nc, nr)), dma((nc,)), dma((nc,)),
            dma((nc, nx - 1)), dma((nc, nx - 1)), dma((nc, 2 * nx)), dma((nc, nr)),
        ],
        compiler_params=pltpu.CompilerParams(
            collective_id=0, has_side_effects=True, vmem_limit_bytes=60 * 1024 * 1024
        ),
    )(inputs, cotangent, preactivation.reshape(nc, ts, hc), up_weight, down_weight)
    for d, piece in enumerate(pieces, 1):
        pieces[d - 1] = lax.ppermute(piece, "col", [(i, (i + d) % nc) for i in range(nc)])
    token_scale = 1.0 / math.sqrt(tokens)
    x_all, cot_all = x_all.reshape(tokens, dr), cot_all.reshape(tokens, dr)
    act_all, pg_all = act_all.reshape(tokens, hc), pg_all.reshape(tokens, hc)
    grad_up = lax.dot_general(x_all, pg_all, FIRST, preferred_element_type=F32) * token_scale
    grad_down = lax.dot_general(act_all, cot_all, FIRST, preferred_element_type=F32) * token_scale
    grad_input = own
    for piece in pieces:
        grad_input += piece.astype(F32)
    grad_input = grad_input.astype(BF16)
    return (grad_input, grad_up, grad_down)


def solution(mesh):
    placed = (
        P(("groups", "col"), "row"),
        P(("groups", "col"), "row"),
        P(("groups", "row"), "col"),
        P("row", "col"),
        P("col", "row"),
    )
    return jax.shard_map(
        functools.partial(per_device, mesh.shape["row"], mesh.shape["col"]),
        mesh=mesh,
        in_specs=placed,
        out_specs=(
            P(("groups", "col"), "row"),
            P(("groups", "row"), "col"),
            P(("groups", "col"), "row"),
        ),
        check_vma=False,
    )
```

```python
import functools
import math

import jax
import jax.numpy as jnp
from jax import lax
from jax.experimental import pallas as pl
from jax.experimental.pallas import tpu as pltpu
from jax.sharding import PartitionSpec as P


F32, BF16 = jnp.float32, jnp.bfloat16
LAST = (((1,), (1,)), ((), ()))
FIRST = (((0,), (0,)), ((), ()))


def tanh_of(v):
    return jnp.tanh(0.7978845608 * (v + 0.044715 * v * v * v))


def gelu_value(values):
    v = values.astype(F32)
    return 0.5 * v * (1.0 + tanh_of(v))


def gelu_slope(values):
    v = values.astype(F32)
    t = tanh_of(v)
    return 0.5 * (1.0 + t) + 0.5 * v * (1.0 - t * t) * 0.7978845608 * (1.0 + 3.0 * 0.044715 * v * v)


def remote(src, dst, send, recv, where):
    return pltpu.make_async_remote_copy(
        src_ref=src, dst_ref=dst, send_sem=send, recv_sem=recv, device_id=where,
        device_id_type=pl.DeviceIdType.MESH,
    )


def block_at(c, t, nc):
    near = jnp.minimum(c, nc - 1 - c)
    step = -((t + 1) // 2) if t % 2 else t // 2
    return jnp.where(t <= 2 * near, c + step, jnp.where(2 * c < nc - 1, t, nc - 1 - t))


def kernel(
    nr, nc,
    x_ref, cot_ref, pre_ref, up_ref, down_ref,
    *rest,
):
    gi_ref, x_out, cot_out, act_out, pg_out, last_out = rest[:6]
    (
    x_all, cot_all, pre_all, act_all, pg_all, up, down, part, h1_out, h1_in, h2_out, h2_in,
    gi_own, gi_out, gi_in,
    loc, cot_s, cot_r, x_s, x_r, pre_s, pre_r, act_s, act_r, h1_s, h1_r, h2_s, h2_r, pg_s, pg_r, gi_s, gi_r,
    ) = rest[6:]
    r, c = lax.axis_index("row"), lax.axis_index("col")
    nx = nr // 2
    x, k = r // 2, r % 2
    mate = {"row": 2 * x + (1 - k)}
    tb, dr = gi_ref.shape
    ts, hc = pg_all.shape[1:]
    hb, db, eb = min(512, hc), min(512, dr), min(256, hc)
    peers = [(x + d) % nx for d in range(1, nx)]
    ends = []

    barrier = pltpu.get_barrier_semaphore()
    for d in range(1, nr):
        pl.semaphore_signal(barrier, inc=1, device_id={"row": (r + d) % nr}, device_id_type=pl.DeviceIdType.MESH)
    for d in range(1, nc):
        pl.semaphore_signal(barrier, inc=1, device_id={"col": (c + d) % nc}, device_id_type=pl.DeviceIdType.MESH)
    local = [
        pltpu.make_async_copy(cot_ref, cot_all.at[c], loc.at[0]),
        pltpu.make_async_copy(down_ref, down, loc.at[1]),
        pltpu.make_async_copy(pre_ref, pre_all.at[pl.ds(r * nc, nc)], loc.at[2]),
        pltpu.make_async_copy(up_ref, up, loc.at[3]),
        pltpu.make_async_copy(x_ref, x_all.at[c], loc.at[4]),
    ]
    for copy in local:
        copy.start()
    pl.semaphore_wait(barrier, nr + nc - 2)

    def line(all_ref, send, recv, direction, j, source):
        return remote(source, all_ref.at[j], send.at[direction, j], recv.at[j],
                      {"col": c + 1 if direction == 0 else c - 1})

    def pass_on(all_ref, send, recv, own_ref, t):
        for direction, j in ((0, c - t), (1, c + t)):
            there = (j >= 0) & (j < nc)
            onward = (c + 1 < nc) if direction == 0 else (c >= 1)
            jj = jnp.clip(j, 0, nc - 1)
            if t > 0:
                @pl.when(there)
                def _():
                    line(all_ref, send, recv, direction, jj, all_ref.at[jj]).wait_recv()

            @pl.when(there & onward)
            def _():
                src = own_ref if t == 0 else all_ref.at[jj]
                line(all_ref, send, recv, direction, jj, src).start()

    def finish_line(all_ref, send, recv):
        for t in range(nc):
            for direction, j in ((0, c - t), (1, c + t)):
                onward = (c + 1 < nc) if direction == 0 else (c >= 1)
                jj = jnp.clip(j, 0, nc - 1)

                @pl.when((j >= 0) & (j < nc) & onward)
                def _():
                    line(all_ref, send, recv, direction, jj, all_ref.at[jj]).wait_send()

    def act_copy(i, index, source_row, target_row):
        unit = act_all.at[source_row * nc + i]
        return remote(unit, unit, act_s.at[i, index], act_r.at[i, source_row], {"row": target_row})

    def act_send(i):
        for n, p in enumerate(peers):
            started(act_copy(i, 1 + n, r, 2 * p + k))
        started(act_copy(i, 0, r, mate_row))

    def act_on(i):
        for n, p in enumerate(peers):
            act_copy(i, 0, 2 * p + k, mate_row).wait_recv()
            started(act_copy(i, nx + n, 2 * p + k, mate_row))

    def pre_copy(i):
        unit = r * nc + i
        return remote(pre_ref.at[i], pre_all.at[unit], pre_s.at[i], pre_r.at[unit // nr],
                      {"row": unit % nr}), unit % nr != r

    def started(copy):
        copy.start()
        ends.append(copy)

    mate_row = 2 * x + (1 - k)
    pass_on(cot_all, cot_s, cot_r, cot_ref, 0)
    for i in range(nc):
        copy, away = pre_copy(i)
        pl.when(away)(copy.start)

    def activate(row):
        steps = hc // eb

        def body(i, _):
            unit, at = row * nc + i // steps, pl.ds(pl.multiple_of((i % steps) * eb, eb), eb)
            act_all[unit, :, at] = gelu_value(pre_all[unit, :, at]).astype(BF16)
            return 0

        lax.fori_loop(0, nc * steps, body, 0)

    def s0(t):
        j = block_at(c, t, nc)
        if t == 0:
            local[0].wait()
            local[1].wait()
        block = cot_all[j]

        def body(i, _):
            at = pl.ds(pl.multiple_of(i * hb, hb), hb)
            got = lax.dot_general(block, down[at, :], LAST, preferred_element_type=F32)
            for s in range(nr):
                part[t, s, :, at] = got[s * ts : (s + 1) * ts]
            return 0

        lax.fori_loop(0, hc // hb, body, 0)
        for p in range(nx):
            h1_out[t, p] = part[t, 2 * p + (1 - k)].astype(BF16)
        started(remote(h1_out.at[t], h1_in.at[t], h1_s.at[t], h1_r.at[t], mate))

    def s1(t):
        remote(h1_out.at[t], h1_in.at[t], h1_s.at[t], h1_r.at[t], mate).wait_recv()
        for i, p in enumerate(peers):
            h2_out[t, i] = (part[t, 2 * p + k] + h1_in[t, p].astype(F32)).astype(BF16)
            started(remote(h2_out.at[t, i], h2_in.at[t, i], h2_s.at[t, i], h2_r.at[t, i],
                           {"row": 2 * p + k}))

    def pg_copy(t, index, source_row, target_row):
        unit = pg_all.at[block_at(c, t, nc) * nr + source_row]
        return remote(unit, unit, pg_s.at[t, index], pg_r.at[t, source_row], {"row": target_row})

    def s2(t):
        for i, p in enumerate(peers):
            remote(h2_out.at[t, i], h2_in.at[t, i], h2_s.at[t, i], h2_r.at[t, i],
                   {"row": 2 * p + k}).wait_recv()
        j = block_at(c, t, nc)
        unit = j * nr + r

        @pl.when(unit // nc != r)
        def _():
            remote(pre_ref.at[0], pre_all.at[unit], pre_s.at[0], pre_r.at[j], mate).wait_recv()

        def body(i, _):
            at = pl.ds(pl.multiple_of(i * eb, eb), eb)
            total = part[t, 2 * x + k, :, at] + h1_in[t, x, :, at].astype(F32)
            for i in range(nx - 1):
                total += h2_in[t, i, :, at].astype(F32)
            pg_all[unit, :, at] = (total * gelu_slope(pre_all[unit, :, at])).astype(BF16)
            return 0

        lax.fori_loop(0, hc // eb, body, 0)
        for i, p in enumerate(peers):
            started(pg_copy(t, 1 + i, r, 2 * p + k))
        started(pg_copy(t, 0, r, mate_row))

    def s3(t):
        for i, p in enumerate(peers):
            pg_copy(t, 0, 2 * p + k, mate_row).wait_recv()
            started(pg_copy(t, nx + i, 2 * p + k, mate_row))

    def gi_copy(t, source):
        return remote(gi_out.at[t], gi_in.at[source], gi_s.at[t], gi_r.at[source],
                      {"col": block_at(c, t, nc)})

    def s4(t):
        j = block_at(c, t, nc)
        for p in range(nx):
            pg_copy(t, 0, 2 * p + (1 - k), mate_row).wait_recv()
        units = pg_all[pl.ds(j * nr, nr)]

        def put(at, rows, got):
            if t == 0:
                gi_own[rows, at] = got
            else:
                gi_out[t, rows, at] = got.astype(BF16)

        def body(i, _):
            at = pl.ds(pl.multiple_of(i * db, db), db)
            if ts % 16 == 0:
                put(at, slice(None), lax.dot_general(
                    units.reshape(tb, hc), up[at, :], LAST, preferred_element_type=F32))
            else:
                got = [lax.dot_general(units[s], up[at, :], LAST, preferred_element_type=F32)
                       for s in range(nr)]
                put(at, slice(None), jnp.concatenate(got, axis=0))
            return 0

        lax.fori_loop(0, dr // db, body, 0)
        if 0 < t < nc - 1:
            started(gi_copy(t, c))

    def out_copy(src, dst, index):
        copy = pltpu.make_async_copy(src, dst, loc.at[index])
        copy.start()
        outs.append(copy)

    outs = []

    def x_on(step):
        for direction, far in ((0, c), (1, nc - 1 - c)):
            t = step - far
            j = c - t if direction == 0 else c + t
            jj = jnp.clip(j, 0, nc - 1)
            fits = (t >= 0) & (t <= far) & (far < nc - 1)

            @pl.when(fits & (t > 0))
            def _():
                line(x_all, x_s, x_r, direction, jj, x_all.at[jj]).wait_recv()

            @pl.when(fits)
            def _():
                line(x_all, x_s, x_r, direction, jj, x_all.at[jj]).start()

    def x_rest():
        for direction, far in ((0, c), (1, nc - 1 - c)):
            for t in range(1, nc):
                j = c - t if direction == 0 else c + t

                @pl.when((far == nc - 1))
                def _():
                    jj = jnp.clip(j, 0, nc - 1)
                    line(x_all, x_s, x_r, direction, jj, x_all.at[jj]).wait_recv()

    early = nc // 2
    local[4].wait()
    for step in range(nc):
        if step == 1:
            local[3].wait()
        if step > 0:
            pass_on(cot_all, cot_s, cot_r, cot_ref, step)
        x_on(step)
        s0(step)
        if step == 0:
            local[2].wait()
            activate(r)
        s1(step)
        if step >= 1:
            s2(step - 1)
        if step < early:
            act_send(step)
        if step >= 2:
            s3(step - 2)
    out_copy(cot_all, cot_out, 5)
    onward = list(range(nc, 2 * nc - 3))
    for at in onward[:1]:
        x_on(at)
    for t in range(1, nc - 2):
        s4(t)
    s2(nc - 1)
    for i in range(early, nc):
        act_send(i)
    s3(nc - 2)
    s4(nc - 2)
    for at in onward[1:]:
        x_on(at)
    s4(0)
    s3(nc - 1)
    s4(nc - 1)
    out_copy(gi_out.at[nc - 1], last_out, 9)
    for i in range(nc):
        act_on(i)
    for i in range(nc):
        for p in range(nx):
            act_copy(i, 0, 2 * p + 1 - k, mate_row).wait_recv()
    out_copy(act_all, act_out, 6)
    out_copy(pg_all, pg_out, 7)
    x_rest()
    out_copy(x_all, x_out, 8)
    gi_ref[...] = gi_own[...]
    for d in range(1, nc):
        source = (c + d) % nc

        @pl.when(block_at(source, nc - 1, nc) != c)
        def _():
            gi_copy(1, source).wait_recv()
            gi_ref[...] += gi_in[source].astype(F32)

    for copy in ends:
        copy.wait_send()
    for i in range(nc):
        copy, away = pre_copy(i)
        pl.when(away)(copy.wait_send)
    finish_line(cot_all, cot_s, cot_r)
    finish_line(x_all, x_s, x_r)
    for copy in outs:
        copy.wait()


def per_device(nr, nc, inputs, cotangent, preactivation, up_weight, down_weight):
    tb, dr = inputs.shape
    hc = up_weight.shape[1]
    ts, nx = tb // nr, nr // 2
    tokens = tb * nc
    dma = pltpu.SemaphoreType.DMA
    anywhere = pl.BlockSpec(memory_space=pl.ANY)
    shape = jax.ShapeDtypeStruct
    own, x_all, cot_all, act_all, pg_all, piece = pl.pallas_call(
        functools.partial(kernel, nr, nc),
        out_shape=(
            shape((tb, dr), F32), shape((nc, tb, dr), BF16), shape((nc, tb, dr), BF16),
            shape((nc * nr, ts, hc), BF16), shape((nc * nr, ts, hc), BF16),
            shape((tb, dr), BF16),
        ),
        in_specs=[anywhere] * 5,
        out_specs=(pl.BlockSpec(memory_space=pltpu.VMEM),) + (anywhere,) * 5,
        scratch_shapes=[
            pltpu.VMEM((nc, tb, dr), BF16), pltpu.VMEM((nc, tb, dr), BF16),
            pltpu.VMEM((nc * nr, ts, hc), BF16), pltpu.VMEM((nc * nr, ts, hc), BF16),
            pltpu.VMEM((nc * nr, ts, hc), BF16),
            pltpu.VMEM(up_weight.shape, BF16), pltpu.VMEM(down_weight.shape, BF16),
            pltpu.VMEM((nc, nr, ts, hc), F32),
            pltpu.VMEM((nc, nx, ts, hc), BF16), pltpu.VMEM((nc, nx, ts, hc), BF16),
            pltpu.VMEM((nc, nx - 1, ts, hc), BF16), pltpu.VMEM((nc, nx - 1, ts, hc), BF16),
            pltpu.VMEM((tb, dr), F32),
            pltpu.VMEM((nc, tb, dr), BF16), pltpu.VMEM((nc, tb, dr), BF16),
            dma((10,)), dma((2, nc)), dma((nc,)), dma((2, nc)), dma((nc,)),
            dma((nc,)), dma((nc,)), dma((nc, 2 * nx)), dma((nc, nr)), dma((nc,)), dma((nc,)),
            dma((nc, nx - 1)), dma((nc, nx - 1)), dma((nc, 2 * nx)), dma((nc, nr)),
            dma((nc,)), dma((nc,)),
        ],
        compiler_params=pltpu.CompilerParams(
            collective_id=0, has_side_effects=True, vmem_limit_bytes=60 * 1024 * 1024
        ),
    )(inputs, cotangent, preactivation.reshape(nc, ts, hc), up_weight, down_weight)
    rounds = []
    for source in range(nc):
        target = nc - 1 if 2 * source <= nc - 1 else 0
        at = next((p for p in rounds if target not in [b for _, b in p]), None)
        if at is None:
            rounds.append(at := [])
        at.append((source, target))
    pieces = [lax.ppermute(piece, "col", pairs) for pairs in rounds]
    token_scale = 1.0 / math.sqrt(tokens)
    x_all, cot_all = x_all.reshape(tokens, dr), cot_all.reshape(tokens, dr)
    act_all, pg_all = act_all.reshape(tokens, hc), pg_all.reshape(tokens, hc)
    grad_up = lax.dot_general(x_all, pg_all, FIRST, preferred_element_type=F32) * token_scale
    grad_down = lax.dot_general(act_all, cot_all, FIRST, preferred_element_type=F32) * token_scale
    grad_input = own
    for piece in pieces:
        grad_input += piece.astype(F32)
    grad_input = grad_input.astype(BF16)
    return (grad_input, grad_up, grad_down)


def solution(mesh):
    placed = (
        P(("groups", "col"), "row"),
        P(("groups", "col"), "row"),
        P(("groups", "row"), "col"),
        P("row", "col"),
        P("col", "row"),
    )
    return jax.shard_map(
        functools.partial(per_device, mesh.shape["row"], mesh.shape["col"]),
        mesh=mesh,
        in_specs=placed,
        out_specs=(
            P(("groups", "col"), "row"),
            P(("groups", "row"), "col"),
            P(("groups", "col"), "row"),
        ),
        check_vma=False,
    )
```
